32 devices in a mesh: sec: 8 (over y, x, core), term: 4 (over z).
Axes of the slice: x: 2, y: 2, z: 4, core: 2. Of those that a mesh axis runs over, the one named last changes fastest.
Arguments:
- meet_env: bfloat16 [8, 24, 256, 256], P('sec', 'term'), may hold values from -0.375 to 0.375
- meet_iso: bfloat16 [8, 256, 2, 256], P('sec'), may hold values from -0.3125 to 0.3125
- last_site: bfloat16 [8, 256, 2, 256], P('sec'), may hold values from -60 to 60
- first_site: bfloat16 [8, 256, 2, 256], P('sec'), may hold values from -0.375 to 0.375
- term_kind: int32 [24, 2], P('term'), may hold values from 0 to 3
Outputs:
- two_site_out: float32 [8, 256, 2, 2, 256], P('sec')
The draws below stay inside these ranges and needn't reach their ends.
All inputs are finite; a program needn't handle non-finite values.
Results may differ from the reference program's by a relative error of at most 0.013.
Values may be sent and summed in bfloat16 or wider, within the bound.
A program may use at most 64 MiB of HBM per device.

```python
import jax
import jax.numpy as jnp
import numpy as np
from jax import lax

BOND = 256
PHYS = 2
TERMS = 24
STEPS = 2
SECS = 8
N_TERM = 4


def draw_last_site(key, part):
    base_key, row_key = jax.random.split(key, 2)
    full_shape = (SECS, BOND, PHYS, BOND)
    base_draw = jax.random.truncated_normal(base_key, -6.0, 6.0, full_shape, jnp.float32)
    row_scale = 10.0 ** jax.random.uniform(row_key, (SECS, BOND, 1, 1), jnp.float32, 0.0, 1.0)
    return (base_draw * row_scale).astype(jnp.bfloat16)


def touch_ends(values, stream_key, smallest, top_value):
    shape = values.shape
    index_at = [jax.random.randint(jax.random.fold_in(stream_key, axis), (), 0, shape[axis]) for axis in range(len(shape))]
    values = values.at[tuple(index_at)].set(smallest)
    longest = shape.index(max(shape))
    index_at[longest] = (index_at[longest] + 1) % shape[longest]
    return values.at[tuple(index_at)].set(top_value)


def shard_levels(rng, extent, shards, low, largest):
    factor_of, own = 1.0, jax.random.fold_in(rng, 6)
    for axis_at, parts in shards:
        heights = jnp.exp(jax.random.uniform(jax.random.fold_in(own, axis_at), (parts,), jnp.float32, low / len(shards), largest / len(shards)))
        factor_of = factor_of * jnp.repeat(heights, extent[axis_at] // parts).reshape([-1 if axis == axis_at else 1 for axis in range(len(extent))])
    return factor_of


def bell_draw(rng, extent, scale, reach, shards=(), kind=jnp.bfloat16):
    drawn = jax.random.normal(rng, extent, jnp.float32) * scale
    if len(shards) > 0:
        drawn = shard_levels(rng, extent, shards, -0.22, 0.18) * drawn
    return jnp.clip(drawn, min=-reach, max=reach).astype(kind)


def setup_inputs(seed: int = 0) -> dict:
    key_list = jax.random.split(jax.random.key(seed), 6)
    meet_env = bell_draw(key_list[0], (SECS, TERMS, BOND, BOND), BOND ** -0.5, 0.375, ((0, 8), (1, 4)))
    meet_iso = bell_draw(key_list[1], (SECS, BOND, PHYS, BOND), (3 * BOND // 2) ** -0.5, 0.3125, ((0, 8),))
    last_site = draw_last_site(jax.random.fold_in(key_list[5], 71), 0)
    first_site = bell_draw(key_list[3], (SECS, BOND, PHYS, BOND), BOND ** -0.5, 0.375, ((0, 8),))
    term_kind = touch_ends(jax.random.randint(key_list[4], (TERMS, 2), 0, 4), jax.random.fold_in(key_list[4], 1), 0, 3).astype(jnp.int32)
    return dict(meet_env=meet_env, meet_iso=meet_iso, last_site=last_site, first_site=first_site, term_kind=term_kind)


operator_table = np.array([[[1.0, 0.0], [0.0, 1.0]], [[0.0, 1.0], [1.0, 0.0]], [[1.0, 0.0], [0.0, -1.0]], [[0.0, 1.0], [-1.0, 0.0]]], dtype=np.float32)
step_size = 0.2
epsilon = 1e-06

def operator_pairs(term_kind):
    levels = jnp.arange(4, dtype=jnp.int32)
    onehot = (term_kind[:, :, None] == levels).astype(jnp.float32)
    return jnp.einsum('kjo,oxy->kjxy', onehot, jnp.asarray(operator_table, dtype=jnp.float32))

def extend(environment, basis, operators):
    wide = jnp.einsum('kab,bsm->kasm', environment.astype(jnp.float32), basis.astype(jnp.float32)).astype(jnp.bfloat16)
    mixed = jnp.einsum('kst,katm->kasm', operators.astype(jnp.float32), wide.astype(jnp.float32)).astype(jnp.bfloat16)
    return jnp.einsum('asm,kasn->kmn', basis.astype(jnp.float32), mixed.astype(jnp.float32)).astype(jnp.bfloat16)

def extend_twice(environment, first_basis, second_basis, operators):
    return extend(extend(environment, first_basis, operators), second_basis, operators)

def apply_terms(vector, left_env, right_env, operators):
    pair_ops = jnp.einsum('ksx,kty->kstxy', operators[:, 0], operators[:, 1]).reshape(operators.shape[0], 4, 4)
    permuted = jnp.einsum('kxy,ayc->kaxc', pair_ops, vector.astype(jnp.float32)).astype(jnp.bfloat16)
    left_applied = jnp.einsum('kab,kbxc->kaxc', left_env.astype(jnp.float32), permuted.astype(jnp.float32)).astype(jnp.bfloat16)
    groups = N_TERM
    per_group = TERMS // N_TERM
    bond_dim = vector.shape[0]
    grouped = jnp.einsum('gkaxc,gkdc->gaxd', left_applied.astype(jnp.float32).reshape(groups, per_group, bond_dim, 4, bond_dim), right_env.astype(jnp.float32).reshape(groups, per_group, bond_dim, bond_dim))
    rounded = lax.optimization_barrier(grouped.astype(jnp.bfloat16))
    return lax.optimization_barrier(jnp.sum(rounded.astype(jnp.float32), axis=0))

def reference(meet_env, meet_iso, last_site, first_site, term_kind):
    operators = operator_pairs(term_kind)
    sections = meet_env.shape[0]
    bond_dim = meet_env.shape[2]

    def fresh_for(section):
        odd_section = section % 2 == 1
        partner = jnp.bitwise_xor(section, 1).astype(jnp.int32)
        partner_iso = meet_iso[partner]
        own_iso = meet_iso[section]
        first_basis = jnp.where(odd_section, partner_iso, jnp.transpose(partner_iso, (2, 1, 0)))
        second_basis = jnp.where(odd_section, own_iso, jnp.transpose(own_iso, (2, 1, 0)))
        chain_ops = jnp.where(odd_section, operators[:, 0], operators[:, 1])
        return extend_twice(meet_env[partner], first_basis, second_basis, chain_ops)
    fresh_env = lax.map(fresh_for, jnp.arange(sections, dtype=jnp.int32))

    def solve_for(section):
        odd_section = section % 2 == 1
        before = ((section + sections - 1) % sections).astype(jnp.int32)
        left_env = jnp.where(odd_section, meet_env[before], fresh_env[before])
        right_env = jnp.where(odd_section, meet_env[section], fresh_env[section])
        two_site = jnp.dot(last_site[before].reshape(2 * bond_dim, bond_dim), first_site[section].reshape(bond_dim, 2 * bond_dim), preferred_element_type=jnp.float32).reshape(bond_dim, 4, bond_dim)
        for step_index in range(STEPS):
            update = apply_terms(two_site.astype(jnp.bfloat16), left_env, right_env, operators)
            two_site = two_site - step_size * update
        norm_scale = lax.rsqrt(jnp.mean(two_site * two_site) + epsilon)
        return (two_site * norm_scale).reshape(bond_dim, PHYS, PHYS, bond_dim)
    return lax.map(solve_for, jnp.arange(sections, dtype=jnp.int32))
```

```python
import functools

import jax
import jax.numpy as jnp
from jax import lax
from jax.experimental import pallas as pl
from jax.experimental.pallas import tpu as pltpu
from jax.sharding import PartitionSpec as P

PHYS = 2
STEPS = 2
PARTS = 4
LAG = 9
GROUP = 2
step_size = 0.2
epsilon = 1e-06
F32 = jnp.float32
BF16 = jnp.bfloat16
MESH = pl.DeviceIdType.MESH


def matmul(lhs, rhs):
    return jnp.dot(lhs, rhs, preferred_element_type=F32)


def kernel(
    n_sec,
    n_term,
    terms,
    kind_ref,
    env_ref,
    iso_ref,
    last_ref,
    first_ref,
    out_ref,
    left,
    rbuf,
    mid,
    came_mid,
    fresh,
    piso,
    came,
    basis,
    table,
    h,
    v,
    two_site,
    acc,
    tot,
    recv,
    one_send,
    one_recv,
    mid_send,
    mid_recv,
    fresh_send,
    fresh_recv,
    in_send,
    chunk_recv,
    out_send,
):
    pairs = PHYS * PHYS
    rows = left.shape[1] // PARTS
    chunks = pairs * PARTS
    sec = lax.axis_index("sec")
    term = lax.axis_index("term")
    odd = lax.rem(sec, 2)
    is_odd = odd == 1
    is_even = odd == 0
    partner = sec + 1 - 2 * odd
    following = lax.rem(sec + 1, n_sec)
    before = lax.rem(sec + n_sec - 1, n_sec)
    ahead = lax.rem(sec + 2, n_sec)
    behind = lax.rem(sec + n_sec - 2, n_sec)
    half = n_term // 2
    left_side = term < half
    inward = jnp.where(left_side, term + 1, term - 1)
    outward = jnp.where(left_side, term - 1, term + 1)
    has_outward = jnp.logical_and(term > 0, term < n_term - 1)
    middle = jnp.logical_or(term == half - 1, term == half)
    in_slot = jnp.where(middle, 1, 0)

    def at(s, t):
        return dict(device_id=(s, t), device_id_type=MESH)

    barrier = pltpu.get_barrier_semaphore()
    pl.semaphore_signal(barrier, inc=1, **at(partner, term))
    pl.semaphore_signal(barrier, inc=1, **at(sec, inward))

    @pl.when(has_outward)
    def _():
        pl.semaphore_signal(barrier, inc=1, **at(sec, outward))

    @pl.when(is_odd)
    def _():
        pl.semaphore_signal(barrier, inc=1, **at(following, term))

    @pl.when(is_even)
    def _():
        for s in (ahead, behind, before):
            pl.semaphore_signal(barrier, inc=1, **at(s, term))

    def remote(src, dst, send, receive, s, t):
        return pltpu.make_async_remote_copy(
            src_ref=src, dst_ref=dst, send_sem=send, recv_sem=receive, **at(s, t)
        )

    iso_copy = remote(iso_ref, piso, one_send.at[0], one_recv.at[0], partner, term)
    last_copy = remote(last_ref, came, one_send.at[1], one_recv.at[1], following, term)
    env_copy = remote(env_ref, left, one_send.at[2], one_recv.at[2], partner, term)

    def mid_copy(k):
        return remote(mid.at[k], came_mid.at[k], mid_send.at[k], mid_recv.at[k], partner, term)

    def block_of(g):
        return pl.ds(pl.multiple_of(g * rows, rows), rows)

    def fresh_first(k):
        return remote(
            fresh.at[k, pl.ds(0, rows)],
            left.at[k, pl.ds(0, rows)],
            fresh_send.at[k],
            fresh_recv.at[k],
            ahead,
            term,
        )

    def fresh_block(g):
        return remote(
            fresh.at[:, block_of(g)],
            left.at[:, block_of(g)],
            fresh_send.at[terms - 1 + g],
            fresh_recv.at[terms - 1 + g],
            ahead,
            term,
        )

    def in_copy(n, x):
        return remote(
            acc.at[n, x],
            recv.at[n, in_slot, x],
            in_send.at[n, x],
            chunk_recv.at[n, in_slot, x],
            sec,
            inward,
        )

    def out_copy(n, x):
        return remote(
            tot.at[n, x],
            recv.at[n, 1, x],
            out_send.at[n, x],
            chunk_recv.at[n, 1, x],
            sec,
            outward,
        )

    def arrived(n, slot, x):
        return remote(
            acc.at[n, x],
            recv.at[n, slot, x],
            in_send.at[n, x],
            chunk_recv.at[n, slot, x],
            sec,
            inward,
        )

    def set_basis(which, source, flip):
        for s in range(PHYS):
            value = source[s]
            turned = value.T
            basis[which, s] = turned if flip else value
            table[which, s] = value if flip else turned
            if s == 1:
                table[which, 2] = -value if flip else -turned

    def extend(values, which, kinds):
        wide = [
            [matmul(value, basis[which, r]).astype(BF16) for r in range(PHYS)] for value in values
        ]
        results = []
        for (wide_0, wide_1), kind in zip(wide, kinds):
            first = jnp.where(kind == 1, 1, jnp.where(kind == 3, 2, 0))
            second = jnp.where(kind == 0, 1, jnp.where(kind == 2, 2, 0))
            result = matmul(table[which, first], wide_0) + matmul(table[which, second], wide_1)
            results.append(result.astype(BF16))
        return results

    group = GROUP if terms % GROUP == 0 else 1

    def own_group(i, carry):
        members = [group * i + m for m in range(group)]
        kinds = [kind_ref[k, odd] for k in members]
        for k, value in zip(members, extend([env_ref[k] for k in members], 0, kinds)):
            mid[k] = value

        @pl.when(is_odd)
        def _():
            for k in members:
                mid_copy(k).start()

        return carry

    @pl.when(is_odd)
    def _():
        set_basis(0, iso_ref, True)

        def turn(k, carry):
            rbuf[k] = env_ref[k].T
            return carry

        lax.fori_loop(0, terms, turn, 0)

    @pl.when(is_even)
    def _():
        set_basis(0, iso_ref, False)
        set_basis(2, iso_ref, True)

    count = 3 + jnp.where(is_even, 2, 0) + jnp.where(has_outward, 1, 0)
    pl.semaphore_wait(barrier, count)

    @pl.when(is_odd)
    def _():
        iso_copy.start()
        last_copy.start()

    @pl.when(is_even)
    def _():
        last_copy.start()
        env_copy.start()

    lax.fori_loop(0, terms // group, own_group, 0)

    @pl.when(is_even)
    def _():
        iso_copy.wait_recv()
        set_basis(1, piso, False)

        def fresh_group(i, carry):
            members = [group * i + m for m in range(group)]
            kinds = [kind_ref[k, 0] for k in members]
            for k, value in zip(members, extend([mid[k] for k in members], 1, kinds)):
                fresh[k] = value
                fresh_first(k).start()
            return carry

        lax.fori_loop(0, terms // group, fresh_group, 0)
        for g in range(1, PARTS):
            fresh_block(g).start()

        def right_group(i, carry):
            members = [group * i + m for m in range(group)]
            for k in members:
                mid_copy(k).wait_recv()
            kinds = [kind_ref[k, 1] for k in members]
            for k, value in zip(members, extend([came_mid[k] for k in members], 2, kinds)):
                rbuf[k] = value.T
            return carry

        lax.fori_loop(0, terms // group, right_group, 0)

    last_copy.wait_recv()
    for s in range(PHYS):
        for t in range(PHYS):
            value = matmul(came[s], first_ref[t])
            for part in range(PARTS):
                piece = value[part * rows : (part + 1) * rows]
                two_site[pairs * part + PHYS * s + t] = piece
                v[pairs * part + PHYS * s + t] = piece.astype(BF16)

    def right_of(n, g):
        lhs = jnp.concatenate([v[pairs * g + x] for x in range(pairs)], axis=0)
        for k in range(terms):
            value = matmul(lhs, rbuf[k]).astype(BF16)
            for x in range(pairs):
                h[n, k, x, block_of(g)] = value[x * rows : (x + 1) * rows]

    def first_right(g, carry):
        right_of(0, g)
        return carry

    lax.fori_loop(0, PARTS, first_right, 0)

    @pl.when(is_odd)
    def _():
        env_copy.wait_recv()

    def wait_block(g):
        @pl.when(g == 0)
        def _():
            for k in range(terms):
                fresh_first(k).wait_recv()

        @pl.when(g > 0)
        def _():
            fresh_block(g).wait_recv()

    def partial_of(n, g):
        if n == 0:

            @pl.when(is_even)
            def _():
                wait_block(g)

        for s in range(PHYS):
            for t in range(PHYS):
                total = None
                for k in range(terms):
                    kind_0, kind_1 = kind_ref[k, 0], kind_ref[k, 1]
                    flip_0, minus_0 = lax.rem(kind_0, 2), kind_0 // 2
                    flip_1, minus_1 = lax.rem(kind_1, 2), kind_1 // 2
                    from_s = flip_0 if s == 0 else 1 - flip_0
                    from_t = flip_1 if t == 0 else 1 - flip_1
                    sign = (1 - 2 * s * minus_0) * (1 - 2 * t * minus_1)
                    lhs = left[k, block_of(g)] * sign.astype(F32).astype(BF16)
                    value = matmul(lhs, h[n, k, PHYS * from_s + from_t])
                    total = value if total is None else total + value
                acc[n, pairs * g + PHYS * s + t] = total.astype(BF16)

    def pass_inward(n, j):
        @pl.when(has_outward)
        def _():
            arrived(n, 0, j).wait_recv()
            acc[n, j] = (acc[n, j].astype(F32) + recv[n, 0, j].astype(F32)).astype(BF16)

        in_copy(n, j).start()

    def pass_outward(n, j, squares):
        arrived(n, 1, j).wait_recv()
        came_in = recv[n, 1, j].astype(F32)
        own = jnp.where(middle, 1.0, 0.0)
        whole = (came_in + own * acc[n, j].astype(F32)).astype(BF16)

        @pl.when(has_outward)
        def _():
            tot[n, j] = whole
            out_copy(n, j).start()

        value = two_site[j] - step_size * whole.astype(F32)
        two_site[j] = value
        if n < STEPS - 1:
            v[j] = value.astype(BF16)
            return squares
        return squares + jnp.sum((value * value).reshape((rows // 8, 8, value.shape[1])), axis=0)

    lag = jnp.where(has_outward, min(LAG, chunks), chunks)
    zero = jnp.zeros((8, two_site.shape[2]), F32)
    for n in range(STEPS):

        def step(j, squares):
            @pl.when(jnp.logical_and(j < chunks, lax.rem(j, pairs) == 0))
            def _():
                partial_of(n, j // pairs)

            @pl.when(j < chunks)
            def _():
                pass_inward(n, j)

            return squares

        def body(j, squares):
            squares = step(j, squares)
            done = j - lag
            squares = pass_outward(n, done, squares)
            if n < STEPS - 1:

                @pl.when(lax.rem(done, pairs) == pairs - 1)
                def _():
                    right_of(n + 1, done // pairs)

            return squares

        lax.fori_loop(0, lag, step, 0)
        squares = lax.fori_loop(lag, chunks + lag, body, zero)

    size = two_site.shape[0] * two_site.shape[1] * two_site.shape[2]
    scale = lax.rsqrt(jnp.full((1, 1), jnp.sum(squares), F32) / size + epsilon)

    lanes = out_ref.shape[1]
    halves = two_site.shape[2] // lanes
    stride = pairs * halves
    for part in range(PARTS):
        for s in range(PHYS):
            for t in range(PHYS):
                for c in range(halves):
                    start = part * rows * stride + (s * halves + c) * PHYS + t
                    columns = pl.ds(c * lanes, lanes)
                    out_ref[pl.ds(start, rows, stride=stride), :] = (
                        two_site[pairs * part + PHYS * s + t, :, columns] * scale
                    )

    last_copy.wait_send()

    @pl.when(is_odd)
    def _():
        iso_copy.wait_send()

        def drain_mid(k, carry):
            mid_copy(k).wait_send()
            return carry

        lax.fori_loop(0, terms, drain_mid, 0)

    @pl.when(is_even)
    def _():
        env_copy.wait_send()

        def drain_fresh(k, carry):
            fresh_first(k).wait_send()
            return carry

        lax.fori_loop(0, terms, drain_fresh, 0)
        for g in range(1, PARTS):
            fresh_block(g).wait_send()

    for n in range(STEPS):

        def drain_chunk(x, carry):
            in_copy(n, x).wait_send()

            @pl.when(has_outward)
            def _():
                out_copy(n, x).wait_send()

            return carry

        lax.fori_loop(0, chunks, drain_chunk, 0)


def shards(n_sec, n_term, meet_env, meet_iso, last_site, first_site, term_kind):
    terms, bond = meet_env.shape[1], meet_env.shape[2]
    pairs = PHYS * PHYS

    def by_level(site):
        return jnp.transpose(site[0], (1, 0, 2))

    vmem = pl.BlockSpec(memory_space=pltpu.VMEM)
    block = (bond, bond)
    chunks = pairs * PARTS
    strip = (bond // PARTS, bond)
    lanes = min(bond, 128)
    dma = pltpu.SemaphoreType.DMA
    out = pl.pallas_call(
        functools.partial(kernel, n_sec, n_term, terms),
        out_shape=jax.ShapeDtypeStruct((pairs * bond * bond // lanes, lanes), F32),
        in_specs=[pl.BlockSpec(memory_space=pltpu.SMEM)] + [vmem] * 4,
        out_specs=vmem,
        scratch_shapes=[
            pltpu.VMEM((terms,) + block, BF16),
            pltpu.VMEM((terms,) + block, BF16),
            pltpu.VMEM((terms,) + block, BF16),
            pltpu.VMEM((terms,) + block, BF16),
            pltpu.VMEM((terms,) + block, BF16),
            pltpu.VMEM((PHYS,) + block, BF16),
            pltpu.VMEM((PHYS,) + block, BF16),
            pltpu.VMEM((3, PHYS) + block, BF16),
            pltpu.VMEM((3, 3) + block, BF16),
            pltpu.VMEM((STEPS, terms, pairs) + block, BF16),
            pltpu.VMEM((chunks,) + strip, BF16),
            pltpu.VMEM((chunks,) + strip, F32),
            pltpu.VMEM((STEPS, chunks) + strip, BF16),
            pltpu.VMEM((STEPS, chunks) + strip, BF16),
            pltpu.VMEM((STEPS, 2, chunks) + strip, BF16),
            dma((3,)),
            dma((3,)),
            dma((terms,)),
            dma((terms,)),
            dma((terms + PARTS - 1,)),
            dma((terms + PARTS - 1,)),
            dma((STEPS, chunks)),
            dma((STEPS, 2, chunks)),
            dma((STEPS, chunks)),
        ],
        compiler_params=pltpu.CompilerParams(
            collective_id=0, has_side_effects=True, vmem_limit_bytes=48 * 1024 * 1024
        ),
    )(term_kind, meet_env[0], by_level(meet_iso), by_level(last_site), by_level(first_site))
    out = out.reshape(bond, PHYS, bond // lanes, PHYS, lanes)
    out = jnp.transpose(out, (0, 1, 3, 2, 4))
    return out.reshape(1, bond, PHYS, PHYS, bond)


def solution(mesh):
    in_specs = (
        P("sec", "term", None, None),
        P("sec", None, None, None),
        P("sec", None, None, None),
        P("sec", None, None, None),
        P("term", None),
    )
    out_specs = P("sec", None, None, None, None)
    body = functools.partial(shards, mesh.shape["sec"], mesh.shape["term"])
    return jax.shard_map(body, mesh=mesh, in_specs=in_specs, out_specs=out_specs, check_vma=False)
```

```python
import functools

import jax
import jax.numpy as jnp
from jax import lax
from jax.experimental import pallas as pl
from jax.experimental.pallas import tpu as pltpu
from jax.sharding import PartitionSpec as P

PHYS = 2
STEPS = 2
PARTS = 4
LAG = 8
GROUP = 2
step_size = 0.2
epsilon = 1e-06
F32 = jnp.float32
BF16 = jnp.bfloat16
MESH = pl.DeviceIdType.MESH


def matmul(lhs, rhs):
    return jnp.dot(lhs, rhs, preferred_element_type=F32)


def kernel(
    n_sec,
    n_term,
    terms,
    kind_hbm,
    env_hbm,
    iso_hbm,
    last_hbm,
    first_hbm,
    out_ref,
    kind_ref,
    env_ref,
    raw,
    sites,
    left,
    rbuf,
    mid,
    came_env,
    fresh,
    piso,
    came,
    basis,
    table,
    h,
    v,
    two_site,
    acc,
    tot,
    recv,
    load,
    one_send,
    one_recv,
    last_send,
    last_recv,
    fresh_send,
    fresh_recv,
    in_send,
    chunk_recv,
    out_send,
):
    pairs = PHYS * PHYS
    rows = left.shape[1] // PARTS
    chunks = pairs * PARTS
    sec = lax.axis_index("sec")
    term = lax.axis_index("term")
    odd = lax.rem(sec, 2)
    is_odd = odd == 1
    is_even = odd == 0
    partner = sec + 1 - 2 * odd
    following = lax.rem(sec + 1, n_sec)
    before = lax.rem(sec + n_sec - 1, n_sec)
    ahead = lax.rem(sec + 2, n_sec)
    behind = lax.rem(sec + n_sec - 2, n_sec)
    half = n_term // 2
    left_side = term < half
    inward = jnp.where(left_side, term + 1, term - 1)
    outward = jnp.where(left_side, term - 1, term + 1)
    has_outward = jnp.logical_and(term > 0, term < n_term - 1)
    middle = jnp.logical_or(term == half - 1, term == half)
    in_slot = jnp.where(middle, 1, 0)
    is_end = jnp.logical_not(has_outward)
    own_level = lax.rem(term, 2)
    beside = term + 1 - 2 * own_level
    iso_ref, last_ref, first_ref = sites.at[0], sites.at[1], sites.at[2]

    def at(s, t):
        return dict(device_id=(s, t), device_id_type=MESH)

    barrier = pltpu.get_barrier_semaphore()
    pl.semaphore_signal(barrier, inc=1, **at(partner, term))
    pl.semaphore_signal(barrier, inc=1, **at(sec, inward))

    @pl.when(has_outward)
    def _():
        pl.semaphore_signal(barrier, inc=1, **at(sec, outward))

    @pl.when(is_even)
    def _():
        for s in (behind, before):
            pl.semaphore_signal(barrier, inc=1, **at(s, term))

    loads = [
        pltpu.make_async_copy(src, dst, load.at[i])
        for i, (src, dst) in enumerate(
            (
                (iso_hbm, raw.at[0]),
                (last_hbm, raw.at[1]),
                (first_hbm, raw.at[2]),
                (kind_hbm, kind_ref),
                (env_hbm, env_ref),
            )
        )
    ]
    for i in (0, 1, 4, 3, 2):
        loads[i].start()

    def remote(src, dst, send, receive, s, t):
        return pltpu.make_async_remote_copy(
            src_ref=src, dst_ref=dst, send_sem=send, recv_sem=receive, **at(s, t)
        )

    iso_copy = remote(iso_ref, piso, one_send.at[0], one_recv.at[0], partner, term)
    env_copy = remote(env_ref, left, one_send.at[1], one_recv.at[1], partner, term)
    side_copy = remote(env_ref, came_env, one_send.at[1], one_recv.at[1], partner, term)

    def last_copy(level):
        return remote(
            last_ref.at[level],
            came.at[level],
            last_send.at[level],
            last_recv.at[level],
            following,
            term,
        )

    def share_copy(level):
        return remote(
            came.at[level], came.at[level], one_send.at[2], last_recv.at[level], sec, beside
        )


    def block_of(g):
        return pl.ds(pl.multiple_of(g * rows, rows), rows)

    def fresh_first(k):
        return remote(
            fresh.at[k, pl.ds(0, rows)],
            left.at[k, pl.ds(0, rows)],
            fresh_send.at[0],
            fresh_recv.at[0],
            ahead,
            term,
        )

    def fresh_block(g):
        return remote(
            fresh.at[:, block_of(g)],
            left.at[:, block_of(g)],
            fresh_send.at[0],
            fresh_recv.at[g],
            ahead,
            term,
        )

    def recv_row(n, slot):
        return slot * (1 + n)

    def in_copy(n, x):
        return remote(
            acc.at[n, x],
            recv.at[n, in_slot, x],
            in_send.at[n],
            chunk_recv.at[recv_row(n, in_slot), x],
            sec,
            inward,
        )

    def out_copy(n, x):
        return remote(
            tot.at[n, x],
            recv.at[n, 1, x],
            out_send.at[n],
            chunk_recv.at[recv_row(n, 1), x],
            sec,
            outward,
        )

    def arrived(n, slot, x):
        return remote(
            acc.at[n, x],
            recv.at[n, slot, x],
            in_send.at[n],
            chunk_recv.at[recv_row(n, slot), x],
            sec,
            inward,
        )

    def set_basis(which, source, flip):
        for s in range(PHYS):
            value = source[s]
            turned = value.T
            basis[which, s] = turned if flip else value
            table[which, s] = value if flip else turned
            if s == 1:
                table[which, 2] = -value if flip else -turned

    def extend(values, which, kinds):
        wide = [
            [matmul(value, basis[which, r]).astype(BF16) for r in range(PHYS)] for value in values
        ]
        results = []
        for (wide_0, wide_1), kind in zip(wide, kinds):
            first = jnp.where(kind == 1, 1, jnp.where(kind == 3, 2, 0))
            second = jnp.where(kind == 0, 1, jnp.where(kind == 2, 2, 0))
            result = matmul(table[which, first], wide_0) + matmul(table[which, second], wide_1)
            results.append(result.astype(BF16))
        return results

    group = GROUP if terms % GROUP == 0 else 1

    def own_group(i, carry):
        members = [group * i + m for m in range(group)]
        kinds = [kind_ref[0, k] for k in members]
        for k, value in zip(members, extend([env_ref[k] for k in members], 0, kinds)):
            mid[k] = value
        return carry

    def split_levels(i):
        sites[i] = jnp.transpose(raw[i], (1, 0, 2))

    loads[0].wait()
    split_levels(0)
    loads[1].wait()
    split_levels(1)
    loads[4].wait()
    loads[3].wait()

    @pl.when(is_odd)
    def _():
        def turn(k, carry):
            rbuf[k] = env_ref[k].T
            return carry

        lax.fori_loop(0, terms, turn, 0)

    @pl.when(is_even)
    def _():
        set_basis(0, iso_ref, False)
        own_group(0, 0)

    pl.semaphore_wait(barrier, 3 + jnp.where(has_outward, 1, 0))

    @pl.when(is_odd)
    def _():
        iso_copy.start()
        last_copy(own_level).start()
        side_copy.start()
        loads[2].wait()
        split_levels(2)

    @pl.when(is_even)
    def _():
        for s in range(PHYS):
            last_copy(s).start()
        env_copy.start()
        lax.fori_loop(1, terms // group, own_group, 0)

    @pl.when(is_even)
    def _():
        iso_copy.wait_recv()
        set_basis(1, piso, False)

        def fresh_group(i, carry):
            members = [group * i + m for m in range(group)]
            kinds = [kind_ref[0, k] for k in members]
            for k, value in zip(members, extend([mid[k] for k in members], 1, kinds)):
                fresh[k] = value
                fresh_first(k).start()
            return carry

        lax.fori_loop(0, terms // group, fresh_group, 0)
        for g in range(1, PARTS):
            fresh_block(g).start()

        def right_group(i, carry):
            members = [group * i + m for m in range(group)]
            kinds = [kind_ref[1, k] for k in members]
            for k, value in zip(members, extend(extend([came_env[k] for k in members], 3, kinds), 2, kinds)):
                rbuf[k] = value.T

            @pl.when(i == 0)
            def _():
                last_copy(own_level).wait_recv()
                share_copy(own_level).start()

            return carry

        set_basis(2, iso_ref, True)
        set_basis(3, piso, True)
        loads[2].wait()
        split_levels(2)
        side_copy.wait_recv()
        lax.fori_loop(0, terms // group, right_group, 0)

    def first_right(i, carry):
        level = jnp.where(is_even, own_level + i - 2 * own_level * i, i)

        @pl.when(jnp.logical_or(is_odd, i > 0))
        def _():
            last_copy(level).wait_recv()

        for t in range(PHYS):
            x = PHYS * level + t
            value = matmul(came[level], first_ref[t])
            rounded = value.astype(BF16)
            for part in range(PARTS):
                two_site[pairs * part + x] = value[part * rows : (part + 1) * rows]
                v[pairs * part + x] = rounded[part * rows : (part + 1) * rows]
            for k in range(terms):
                h[0, k, x] = matmul(rounded, rbuf[k]).astype(BF16)
        return carry

    lax.fori_loop(0, PHYS, first_right, 0)

    def right_of(n, g):
        lhs = jnp.concatenate([v[pairs * g + x] for x in range(pairs)], axis=0)
        for k in range(terms):
            value = matmul(lhs, rbuf[k]).astype(BF16)
            for x in range(pairs):
                h[n, k, x, block_of(g)] = value[x * rows : (x + 1) * rows]

    @pl.when(is_odd)
    def _():
        env_copy.wait_recv()

    def wait_block(g):
        fresh_block(g).wait_recv()

    def chunk_sum(n, g, s, t):
        total = None
        for k in range(terms):
            kind_0, kind_1 = kind_ref[0, k], kind_ref[1, k]
            flip_0, minus_0 = lax.rem(kind_0, 2), kind_0 // 2
            flip_1, minus_1 = lax.rem(kind_1, 2), kind_1 // 2
            from_s = s + flip_0 - 2 * s * flip_0
            from_t = t + flip_1 - 2 * t * flip_1
            sign = (1 - 2 * s * minus_0) * (1 - 2 * t * minus_1)
            lhs = left[k, block_of(g)] * sign.astype(F32).astype(BF16)
            value = matmul(lhs, h[n, k, PHYS * from_s + from_t])
            total = value if total is None else total + value
        return total.astype(BF16)

    def partial_of(n, g):
        if n == 0:

            @pl.when(is_even)
            def _():
                wait_block(g)

        for s in range(PHYS):
            for t in range(PHYS):
                acc[n, pairs * g + PHYS * s + t] = chunk_sum(n, g, s, t)

    def send_partial(n, j):
        x = lax.rem(j, pairs)
        if n == 0:

            @pl.when(jnp.logical_and(is_even, x == 0))
            def _():
                wait_block(j // pairs)

        acc[n, j] = chunk_sum(n, j // pairs, x // PHYS, lax.rem(x, PHYS))
        in_copy(n, j).start()

    def pass_inward(n, j):
        arrived(n, 0, j).wait_recv()
        acc[n, j] = (acc[n, j].astype(F32) + recv[n, 0, j].astype(F32)).astype(BF16)
        in_copy(n, j).start()

    def pass_outward(n, j, squares):
        arrived(n, 1, j).wait_recv()
        came_in = recv[n, 1, j].astype(F32)
        own = jnp.where(middle, 1.0, 0.0)
        whole = (came_in + own * acc[n, j].astype(F32)).astype(BF16)

        @pl.when(has_outward)
        def _():
            tot[n, j] = whole
            out_copy(n, j).start()

        value = two_site[j] - step_size * whole.astype(F32)
        two_site[j] = value
        if n < STEPS - 1:
            v[j] = value.astype(BF16)
            return squares
        return squares + jnp.sum((value * value).reshape((rows // 8, 8, value.shape[1])), axis=0)

    lag = jnp.where(has_outward, min(LAG, chunks), chunks)
    begin = jnp.where(has_outward, 0, chunks)
    zero = jnp.zeros((8, two_site.shape[2]), F32)
    for n in range(STEPS):
        gated = jnp.logical_and(is_even, has_outward) if n == 0 else False
        ready = jnp.where(jnp.logical_or(gated, is_end), 0, PARTS)
        sending = jnp.where(is_end, chunks, 0)

        def ahead_of(g, carry):
            partial_of(n, g)
            return carry

        def sent(j, carry):
            send_partial(n, j)
            return carry

        def step(j, squares):
            @pl.when(j < chunks)
            def _():
                if n == 0:

                    @pl.when(jnp.logical_and(gated, lax.rem(j, pairs) == 0))
                    def _():
                        partial_of(n, j // pairs)

                pass_inward(n, j)

            return squares

        def body(j, squares):
            squares = step(j, squares)
            done = j - lag
            squares = pass_outward(n, done, squares)
            if n < STEPS - 1:

                @pl.when(lax.rem(done, pairs) == pairs - 1)
                def _():
                    right_of(n + 1, done // pairs)

            return squares

        lax.fori_loop(0, ready, ahead_of, 0)
        lax.fori_loop(0, sending, sent, 0)
        lax.fori_loop(begin, lag, step, 0)
        squares = lax.fori_loop(lag, chunks + lag, body, zero)

    size = two_site.shape[0] * two_site.shape[1] * two_site.shape[2]
    scale = lax.rsqrt(jnp.full((1, 1), jnp.sum(squares), F32) / size + epsilon)

    lanes = out_ref.shape[1]
    halves = two_site.shape[2] // lanes
    stride = pairs * halves
    for part in range(PARTS):
        for s in range(PHYS):
            for t in range(PHYS):
                for c in range(halves):
                    start = part * rows * stride + (s * halves + c) * PHYS + t
                    columns = pl.ds(c * lanes, lanes)
                    out_ref[pl.ds(start, rows, stride=stride), :] = (
                        two_site[pairs * part + PHYS * s + t, :, columns] * scale
                    )


    @pl.when(is_odd)
    def _():
        iso_copy.wait_send()
        last_copy(own_level).wait_send()
        side_copy.wait_send()

    @pl.when(is_even)
    def _():
        for s in range(PHYS):
            last_copy(s).wait_send()
        env_copy.wait_send()
        share_copy(own_level).wait_send()

        remote(fresh, left, fresh_send.at[0], fresh_recv.at[0], ahead, term).wait_send()

    for n in range(STEPS):
        remote(
            acc.at[n], recv.at[n, 0], in_send.at[n], chunk_recv.at[0, 0], sec, inward
        ).wait_send()

        @pl.when(has_outward)
        def _():
            remote(
                tot.at[n], recv.at[n, 0], out_send.at[n], chunk_recv.at[0, 0], sec, outward
            ).wait_send()


def shards(n_sec, n_term, meet_env, meet_iso, last_site, first_site, term_kind):
    terms, bond = meet_env.shape[1], meet_env.shape[2]
    pairs = PHYS * PHYS

    vmem = pl.BlockSpec(memory_space=pltpu.VMEM)
    block = (bond, bond)
    chunks = pairs * PARTS
    strip = (bond // PARTS, bond)
    lanes = min(bond, 128)
    dma = pltpu.SemaphoreType.DMA
    out = pl.pallas_call(
        functools.partial(kernel, n_sec, n_term, terms),
        out_shape=jax.ShapeDtypeStruct((pairs * bond * bond // lanes, lanes), F32),
        in_specs=[pl.BlockSpec(memory_space=pltpu.HBM)] * 5,
        out_specs=vmem,
        scratch_shapes=[
            pltpu.SMEM(term_kind.shape[::-1], jnp.int32),
            pltpu.VMEM((terms,) + block, BF16),
            pltpu.VMEM((3, bond, PHYS, bond), BF16),
            pltpu.VMEM((3, PHYS) + block, BF16),
            pltpu.VMEM((terms,) + block, BF16),
            pltpu.VMEM((terms,) + block, BF16),
            pltpu.VMEM((terms,) + block, BF16),
            pltpu.VMEM((terms,) + block, BF16),
            pltpu.VMEM((terms,) + block, BF16),
            pltpu.VMEM((PHYS,) + block, BF16),
            pltpu.VMEM((PHYS,) + block, BF16),
            pltpu.VMEM((4, PHYS) + block, BF16),
            pltpu.VMEM((4, 3) + block, BF16),
            pltpu.VMEM((STEPS, terms, pairs) + block, BF16),
            pltpu.VMEM((chunks,) + strip, BF16),
            pltpu.VMEM((chunks,) + strip, F32),
            pltpu.VMEM((STEPS, chunks) + strip, BF16),
            pltpu.VMEM((STEPS, chunks) + strip, BF16),
            pltpu.VMEM((STEPS, 2, chunks) + strip, BF16),
            dma((5,)),
            dma((3,)),
            dma((2,)),
            dma((PHYS,)),
            dma((PHYS,)),
            dma((1,)),
            dma((PARTS,)),
            dma((STEPS,)),
            dma((1 + STEPS, chunks)),
            dma((STEPS,)),
        ],
        compiler_params=pltpu.CompilerParams(
            collective_id=0, has_side_effects=True, vmem_limit_bytes=48 * 1024 * 1024
        ),
    )(*(pltpu.with_memory_space_constraint(a, pltpu.HBM) for a in (term_kind.T, meet_env[0], meet_iso[0], last_site[0], first_site[0])))
    out = out.reshape(bond, PHYS, bond // lanes, PHYS, lanes)
    out = jnp.transpose(out, (0, 1, 3, 2, 4))
    return out.reshape(1, bond, PHYS, PHYS, bond)


def solution(mesh):
    in_specs = (
        P("sec", "term", None, None),
        P("sec", None, None, None),
        P("sec", None, None, None),
        P("sec", None, None, None),
        P("term", None),
    )
    out_specs = P("sec", None, None, None, None)
    body = functools.partial(shards, mesh.shape["sec"], mesh.shape["term"])
    return jax.shard_map(body, mesh=mesh, in_specs=in_specs, out_specs=out_specs, check_vma=False)
```

```python
import functools

import jax
import jax.numpy as jnp
from jax import lax
from jax.experimental import pallas as pl
from jax.experimental.pallas import tpu as pltpu
from jax.sharding import PartitionSpec as P

PHYS = 2
STEPS = 2
PARTS = 4
LAG = 8
GROUP = 6
SIDE = 6
step_size = 0.2
epsilon = 1e-06
F32 = jnp.float32
BF16 = jnp.bfloat16
MESH = pl.DeviceIdType.MESH


def matmul(lhs, rhs):
    return jnp.dot(lhs, rhs, preferred_element_type=F32)


def kernel(
    n_sec,
    n_term,
    terms,
    kind_hbm,
    env_hbm,
    iso_hbm,
    last_hbm,
    first_hbm,
    out_ref,
    kind_ref,
    env_ref,
    raw,
    sites,
    left,
    rbuf,
    mid,
    came_env,
    fresh,
    piso,
    came,
    basis,
    table,
    h,
    v,
    two_site,
    acc,
    tot,
    recv,
    load,
    one_send,
    one_recv,
    last_send,
    last_recv,
    fresh_send,
    fresh_recv,
    in_send,
    chunk_recv,
    out_send,
):
    pairs = PHYS * PHYS
    rows = left.shape[1] // PARTS
    chunks = pairs * PARTS
    sec = lax.axis_index("sec")
    term = lax.axis_index("term")
    odd = lax.rem(sec, 2)
    is_odd = odd == 1
    is_even = odd == 0
    partner = sec + 1 - 2 * odd
    following = lax.rem(sec + 1, n_sec)
    before = lax.rem(sec + n_sec - 1, n_sec)
    ahead = lax.rem(sec + 2, n_sec)
    behind = lax.rem(sec + n_sec - 2, n_sec)
    half = n_term // 2
    left_side = term < half
    inward = jnp.where(left_side, term + 1, term - 1)
    outward = jnp.where(left_side, term - 1, term + 1)
    has_outward = jnp.logical_and(term > 0, term < n_term - 1)
    middle = jnp.logical_or(term == half - 1, term == half)
    in_slot = jnp.where(middle, 1, 0)
    is_end = jnp.logical_not(has_outward)
    own_level = lax.rem(term, 2)
    beside = term + 1 - 2 * own_level
    iso_ref, last_ref, first_ref = sites.at[0], sites.at[1], sites.at[2]

    def at(s, t):
        return dict(device_id=(s, t), device_id_type=MESH)

    barrier = pltpu.get_barrier_semaphore()
    pl.semaphore_signal(barrier, inc=1, **at(partner, term))
    pl.semaphore_signal(barrier, inc=1, **at(sec, inward))

    @pl.when(has_outward)
    def _():
        pl.semaphore_signal(barrier, inc=1, **at(sec, outward))

    @pl.when(is_even)
    def _():
        for s in (behind, before):
            pl.semaphore_signal(barrier, inc=1, **at(s, term))

    loads = [
        pltpu.make_async_copy(src, dst, load.at[i])
        for i, (src, dst) in enumerate(
            (
                (iso_hbm, raw.at[0]),
                (last_hbm, raw.at[1]),
                (first_hbm, raw.at[2]),
                (kind_hbm, kind_ref),
                (env_hbm, env_ref),
            )
        )
    ]
    for i in (0, 1, 4, 3, 2):
        loads[i].start()

    def remote(src, dst, send, receive, s, t):
        return pltpu.make_async_remote_copy(
            src_ref=src, dst_ref=dst, send_sem=send, recv_sem=receive, **at(s, t)
        )

    iso_copy = remote(iso_ref, piso, one_send.at[0], one_recv.at[0], partner, term)
    env_copy = remote(env_ref, left, one_send.at[1], one_recv.at[1], partner, term)
    side_copy = remote(env_ref, came_env, one_send.at[1], one_recv.at[1], partner, term)

    last_whole = remote(last_ref, came, last_send.at[0], last_recv.at[0], partner, term)
    kept = left.shape[1] - rows

    def half_of(site, level, upper):
        return site.at[level, pl.ds(kept, rows) if upper else pl.ds(0, kept)]

    last_parts = [
        remote(
            half_of(last_ref, level, upper),
            half_of(came, level, upper),
            last_send.at[i],
            last_recv.at[i],
            following,
            term,
        )
        for i, (level, upper) in enumerate(
            ((own_level, True), (own_level, False), (1 - own_level, False))
        )
    ]
    share_copy = remote(
        half_of(came, own_level, True),
        half_of(came, own_level, True),
        one_send.at[2],
        last_recv.at[3],
        sec,
        beside,
    )

    def block_of(g):
        return pl.ds(pl.multiple_of(g * rows, rows), rows)

    def fresh_first(k):
        return remote(
            fresh.at[k, pl.ds(0, rows)],
            left.at[k, pl.ds(0, rows)],
            fresh_send.at[0],
            fresh_recv.at[0],
            ahead,
            term,
        )

    def fresh_block(g):
        return remote(
            fresh.at[:, block_of(g)],
            left.at[:, block_of(g)],
            fresh_send.at[0],
            fresh_recv.at[g],
            ahead,
            term,
        )

    def recv_row(n, slot):
        return slot * (1 + n)

    def in_copy(n, x):
        return remote(
            acc.at[n, x],
            recv.at[n, in_slot, x],
            in_send.at[n],
            chunk_recv.at[recv_row(n, in_slot), x],
            sec,
            inward,
        )

    def out_copy(n, x):
        return remote(
            tot.at[n, x],
            recv.at[n, 1, x],
            out_send.at[n],
            chunk_recv.at[recv_row(n, 1), x],
            sec,
            outward,
        )

    def arrived(n, slot, x):
        return remote(
            acc.at[n, x],
            recv.at[n, slot, x],
            in_send.at[n],
            chunk_recv.at[recv_row(n, slot), x],
            sec,
            inward,
        )

    def set_basis(which, source, flip):
        for s in range(PHYS):
            value = source[s]
            turned = value.T
            basis[which, s] = turned if flip else value
            table[which, s] = value if flip else turned
            if s == 1:
                table[which, 2] = -value if flip else -turned

    def extend(values, which, kinds):
        wide = [
            [matmul(value, basis[which, r]).astype(BF16) for r in range(PHYS)] for value in values
        ]
        results = []
        for (wide_0, wide_1), kind in zip(wide, kinds):
            first = jnp.where(kind == 1, 1, jnp.where(kind == 3, 2, 0))
            second = jnp.where(kind == 0, 1, jnp.where(kind == 2, 2, 0))
            result = matmul(table[which, first], wide_0) + matmul(table[which, second], wide_1)
            results.append(result.astype(BF16))
        return results

    group = GROUP if terms % GROUP == 0 else 1
    side_group = SIDE if terms % SIDE == 0 else 1

    def own_group(i, carry):
        members = [group * i + m for m in range(group)]
        kinds = [kind_ref[0, k] for k in members]
        for k, value in zip(members, extend([env_ref[k] for k in members], 0, kinds)):
            mid[k] = value
        return carry

    def split_levels(i):
        sites[i] = jnp.transpose(raw[i], (1, 0, 2))

    loads[0].wait()
    split_levels(0)
    loads[1].wait()
    split_levels(1)

    pl.semaphore_wait(barrier, 3 + jnp.where(has_outward, 1, 0))

    @pl.when(is_odd)
    def _():
        iso_copy.start()
        for copy in last_parts:
            copy.start()

    @pl.when(is_even)
    def _():
        last_whole.start()

    loads[4].wait()

    @pl.when(is_odd)
    def _():
        side_copy.start()

        def turn(k, carry):
            rbuf[k] = env_ref[k].T
            return carry

        lax.fori_loop(0, terms, turn, 0)

    @pl.when(is_even)
    def _():
        env_copy.start()

    loads[3].wait()

    @pl.when(is_even)
    def _():
        set_basis(0, iso_ref, False)
        lax.fori_loop(0, terms // group, own_group, 0)

    @pl.when(is_odd)
    def _():
        loads[2].wait()
        split_levels(2)

    @pl.when(is_even)
    def _():
        iso_copy.wait_recv()
        set_basis(1, piso, False)

        def fresh_group(i, carry):
            members = [group * i + m for m in range(group)]
            kinds = [kind_ref[0, k] for k in members]
            for k, value in zip(members, extend([mid[k] for k in members], 1, kinds)):
                fresh[k] = value
                fresh_first(k).start()
            return carry

        lax.fori_loop(0, terms // group, fresh_group, 0)
        for g in range(1, PARTS):
            fresh_block(g).start()

        def right_group(i, carry):
            members = [side_group * i + m for m in range(side_group)]
            kinds = [kind_ref[1, k] for k in members]
            for k, value in zip(members, extend(extend([came_env[k] for k in members], 3, kinds), 2, kinds)):
                rbuf[k] = value.T

            @pl.when(i == 0)
            def _():
                last_parts[0].wait_recv()
                share_copy.start()

            return carry

        set_basis(2, iso_ref, True)
        set_basis(3, piso, True)
        loads[2].wait()
        split_levels(2)
        side_copy.wait_recv()
        lax.fori_loop(0, terms // side_group, right_group, 0)

    def first_right(i, carry):
        level = jnp.where(is_even, own_level + i - 2 * own_level * i, i)

        @pl.when(jnp.logical_and(is_odd, i == 0))
        def _():
            last_whole.wait_recv()

        @pl.when(jnp.logical_and(is_even, i == 0))
        def _():
            last_parts[1].wait_recv()

        @pl.when(jnp.logical_and(is_even, i > 0))
        def _():
            last_parts[2].wait_recv()
            remote(
                half_of(came, 1 - own_level, True),
                half_of(came, 1 - own_level, True),
                one_send.at[2],
                last_recv.at[3],
                sec,
                beside,
            ).wait_recv()

        for t in range(PHYS):
            x = PHYS * level + t
            value = matmul(came[level], first_ref[t])
            rounded = value.astype(BF16)
            for part in range(PARTS):
                two_site[pairs * part + x] = value[part * rows : (part + 1) * rows]
                v[pairs * part + x] = rounded[part * rows : (part + 1) * rows]
            for k in range(terms):
                h[0, k, x] = matmul(rounded, rbuf[k]).astype(BF16)
        return carry

    lax.fori_loop(0, PHYS, first_right, 0)

    def right_of(n, g):
        lhs = jnp.concatenate([v[pairs * g + x] for x in range(pairs)], axis=0)
        for k in range(terms):
            value = matmul(lhs, rbuf[k]).astype(BF16)
            for x in range(pairs):
                h[n, k, x, block_of(g)] = value[x * rows : (x + 1) * rows]

    @pl.when(is_odd)
    def _():
        env_copy.wait_recv()

    def wait_block(g):
        fresh_block(g).wait_recv()

    def chunk_sum(n, g, s, t):
        total = None
        for k in range(terms):
            kind_0, kind_1 = kind_ref[0, k], kind_ref[1, k]
            flip_0, minus_0 = lax.rem(kind_0, 2), kind_0 // 2
            flip_1, minus_1 = lax.rem(kind_1, 2), kind_1 // 2
            from_s = s + flip_0 - 2 * s * flip_0
            from_t = t + flip_1 - 2 * t * flip_1
            sign = (1 - 2 * s * minus_0) * (1 - 2 * t * minus_1)
            lhs = left[k, block_of(g)] * sign.astype(F32).astype(BF16)
            value = matmul(lhs, h[n, k, PHYS * from_s + from_t])
            total = value if total is None else total + value
        return total.astype(BF16)

    def partial_of(n, g):
        if n == 0:

            @pl.when(is_even)
            def _():
                wait_block(g)

        for s in range(PHYS):
            for t in range(PHYS):
                acc[n, pairs * g + PHYS * s + t] = chunk_sum(n, g, s, t)

    def send_partial(n, j):
        x = lax.rem(j, pairs)
        if n == 0:

            @pl.when(jnp.logical_and(is_even, x == 0))
            def _():
                wait_block(j // pairs)

        acc[n, j] = chunk_sum(n, j // pairs, x // PHYS, lax.rem(x, PHYS))
        in_copy(n, j).start()

    lanes = out_ref.shape[1]
    halves = two_site.shape[2] // lanes
    stride = pairs * halves

    def pass_inward(n, j):
        arrived(n, 0, j).wait_recv()
        acc[n, j] = (acc[n, j].astype(F32) + recv[n, 0, j].astype(F32)).astype(BF16)
        in_copy(n, j).start()

    def pass_outward(n, j, squares):
        arrived(n, 1, j).wait_recv()
        came_in = recv[n, 1, j].astype(F32)
        own = jnp.where(middle, 1.0, 0.0)
        whole = (came_in + own * acc[n, j].astype(F32)).astype(BF16)

        @pl.when(has_outward)
        def _():
            tot[n, j] = whole
            out_copy(n, j).start()

        value = two_site[j] - step_size * whole.astype(F32)
        if n < STEPS - 1:
            two_site[j] = value
            v[j] = value.astype(BF16)
            return squares
        x = lax.rem(j, pairs)
        start = (j // pairs) * (rows * stride) + (x // PHYS) * (halves * PHYS) + lax.rem(x, PHYS)
        for c in range(halves):
            out_ref[pl.ds(start + c * PHYS, rows, stride=stride), :] = value[
                :, c * lanes : (c + 1) * lanes
            ]
        return squares + jnp.sum((value * value).reshape((rows // 8, 8, value.shape[1])), axis=0)

    lag = jnp.where(has_outward, min(LAG, chunks), chunks)
    begin = jnp.where(has_outward, 0, chunks)
    zero = jnp.zeros((8, two_site.shape[2]), F32)
    for n in range(STEPS):
        gated = jnp.logical_and(is_even, has_outward) if n == 0 else False
        ready = jnp.where(is_end, 0, jnp.where(gated, 1, PARTS))
        sending = jnp.where(is_end, chunks, 0)

        def ahead_of(g, carry):
            partial_of(n, g)
            return carry

        def sent(j, carry):
            send_partial(n, j)
            return carry

        def step(j, squares):
            @pl.when(j < chunks)
            def _():
                if n == 0:

                    @pl.when(
                        jnp.logical_and(
                            gated, jnp.logical_and(lax.rem(j, pairs) == 0, j < chunks - pairs)
                        )
                    )
                    def _():
                        partial_of(n, j // pairs + 1)

                pass_inward(n, j)

            return squares

        def body(j, squares):
            squares = step(j, squares)
            done = j - lag
            squares = pass_outward(n, done, squares)
            if n < STEPS - 1:

                @pl.when(lax.rem(done, pairs) == pairs - 1)
                def _():
                    right_of(n + 1, done // pairs)

            return squares

        lax.fori_loop(0, ready, ahead_of, 0)
        lax.fori_loop(0, sending, sent, 0)
        lax.fori_loop(begin, lag, step, 0)
        squares = lax.fori_loop(lag, chunks + lag, body, zero)

    size = two_site.shape[0] * two_site.shape[1] * two_site.shape[2]
    scale = lax.rsqrt(jnp.full((1, 1), jnp.sum(squares), F32) / size + epsilon)

    out_ref[...] = out_ref[...] * scale


    @pl.when(is_odd)
    def _():
        iso_copy.wait_send()
        for copy in last_parts:
            copy.wait_send()
        side_copy.wait_send()

    @pl.when(is_even)
    def _():
        last_whole.wait_send()
        env_copy.wait_send()
        share_copy.wait_send()

        remote(fresh, left, fresh_send.at[0], fresh_recv.at[0], ahead, term).wait_send()

    for n in range(STEPS):
        remote(
            acc.at[n], recv.at[n, 0], in_send.at[n], chunk_recv.at[0, 0], sec, inward
        ).wait_send()

        @pl.when(has_outward)
        def _():
            remote(
                tot.at[n], recv.at[n, 0], out_send.at[n], chunk_recv.at[0, 0], sec, outward
            ).wait_send()


def shards(n_sec, n_term, meet_env, meet_iso, last_site, first_site, term_kind):
    terms, bond = meet_env.shape[1], meet_env.shape[2]
    pairs = PHYS * PHYS

    vmem = pl.BlockSpec(memory_space=pltpu.VMEM)
    block = (bond, bond)
    chunks = pairs * PARTS
    strip = (bond // PARTS, bond)
    lanes = min(bond, 128)
    dma = pltpu.SemaphoreType.DMA
    out = pl.pallas_call(
        functools.partial(kernel, n_sec, n_term, terms),
        out_shape=jax.ShapeDtypeStruct((pairs * bond * bond // lanes, lanes), F32),
        in_specs=[pl.BlockSpec(memory_space=pltpu.HBM)] * 5,
        out_specs=vmem,
        scratch_shapes=[
            pltpu.SMEM(term_kind.shape[::-1], jnp.int32),
            pltpu.VMEM((terms,) + block, BF16),
            pltpu.VMEM((3, bond, PHYS, bond), BF16),
            pltpu.VMEM((3, PHYS) + block, BF16),
            pltpu.VMEM((terms,) + block, BF16),
            pltpu.VMEM((terms,) + block, BF16),
            pltpu.VMEM((terms,) + block, BF16),
            pltpu.VMEM((terms,) + block, BF16),
            pltpu.VMEM((terms,) + block, BF16),
            pltpu.VMEM((PHYS,) + block, BF16),
            pltpu.VMEM((PHYS,) + block, BF16),
            pltpu.VMEM((4, PHYS) + block, BF16),
            pltpu.VMEM((4, 3) + block, BF16),
            pltpu.VMEM((STEPS, terms, pairs) + block, BF16),
            pltpu.VMEM((chunks,) + strip, BF16),
            pltpu.VMEM((chunks,) + strip, F32),
            pltpu.VMEM((STEPS, chunks) + strip, BF16),
            pltpu.VMEM((STEPS, chunks) + strip, BF16),
            pltpu.VMEM((STEPS, 2, chunks) + strip, BF16),
            dma((5,)),
            dma((3,)),
            dma((2,)),
            dma((3,)),
            dma((4,)),
            dma((1,)),
            dma((PARTS,)),
            dma((STEPS,)),
            dma((1 + STEPS, chunks)),
            dma((STEPS,)),
        ],
        compiler_params=pltpu.CompilerParams(
            collective_id=0, has_side_effects=True, vmem_limit_bytes=48 * 1024 * 1024
        ),
    )(*(pltpu.with_memory_space_constraint(a, pltpu.HBM) for a in (term_kind.T, meet_env[0], meet_iso[0], last_site[0], first_site[0])))
    out = out.reshape(bond, PHYS, bond // lanes, PHYS, lanes)
    out = jnp.transpose(out, (0, 1, 3, 2, 4))
    return out.reshape(1, bond, PHYS, PHYS, bond)


def solution(mesh):
    in_specs = (
        P("sec", "term", None, None),
        P("sec", None, None, None),
        P("sec", None, None, None),
        P("sec", None, None, None),
        P("term", None),
    )
    out_specs = P("sec", None, None, None, None)
    body = functools.partial(shards, mesh.shape["sec"], mesh.shape["term"])
    return jax.shard_map(body, mesh=mesh, in_specs=in_specs, out_specs=out_specs, check_vma=False)
```

```python
import functools

import jax
import jax.numpy as jnp
from jax import lax
from jax.experimental import pallas as pl
from jax.experimental.pallas import tpu as pltpu
from jax.sharding import PartitionSpec as P

PHYS = 2
STEPS = 2
PARTS = 4
LAG = 8
GROUP = 6
SIDE = 6
step_size = 0.2
epsilon = 1e-06
F32 = jnp.float32
BF16 = jnp.bfloat16
MESH = pl.DeviceIdType.MESH


def matmul(lhs, rhs):
    return jnp.dot(lhs, rhs, preferred_element_type=F32)


def kernel(
    n_sec,
    n_term,
    terms,
    kind_hbm,
    env_hbm,
    iso_hbm,
    last_hbm,
    first_hbm,
    out_ref,
    kind_ref,
    env_ref,
    raw,
    sites,
    left,
    rbuf,
    mid,
    came_env,
    fresh,
    piso,
    came,
    basis,
    table,
    h,
    v,
    two_site,
    acc,
    tot,
    recv,
    load,
    one_send,
    one_recv,
    last_send,
    last_recv,
    fresh_send,
    fresh_recv,
    in_send,
    chunk_recv,
    out_send,
):
    pairs = PHYS * PHYS
    rows = left.shape[1] // PARTS
    chunks = pairs * PARTS
    sec = lax.axis_index("sec")
    term = lax.axis_index("term")
    odd = lax.rem(sec, 2)
    is_odd = odd == 1
    is_even = odd == 0
    partner = sec + 1 - 2 * odd
    following = lax.rem(sec + 1, n_sec)
    before = lax.rem(sec + n_sec - 1, n_sec)
    ahead = lax.rem(sec + 2, n_sec)
    behind = lax.rem(sec + n_sec - 2, n_sec)
    half = n_term // 2
    left_side = term < half
    inward = jnp.where(left_side, term + 1, term - 1)
    outward = jnp.where(left_side, term - 1, term + 1)
    has_outward = jnp.logical_and(term > 0, term < n_term - 1)
    middle = jnp.logical_or(term == half - 1, term == half)
    in_slot = jnp.where(middle, 1, 0)
    is_end = jnp.logical_not(has_outward)
    own_level = lax.rem(term, 2)
    beside = term + 1 - 2 * own_level
    iso_ref, last_ref, first_ref = sites.at[0], sites.at[1], sites.at[2]

    def at(s, t):
        return dict(device_id=(s, t), device_id_type=MESH)

    barrier = pltpu.get_barrier_semaphore()
    pl.semaphore_signal(barrier, inc=1, **at(partner, term))
    pl.semaphore_signal(barrier, inc=1, **at(sec, inward))

    @pl.when(has_outward)
    def _():
        pl.semaphore_signal(barrier, inc=1, **at(sec, outward))

    @pl.when(is_even)
    def _():
        for s in (behind, before):
            pl.semaphore_signal(barrier, inc=1, **at(s, term))

    loads = [
        pltpu.make_async_copy(src, dst, load.at[i])
        for i, (src, dst) in enumerate(
            (
                (iso_hbm, raw.at[0]),
                (last_hbm, raw.at[1]),
                (first_hbm, raw.at[2]),
                (kind_hbm, kind_ref),
                (env_hbm, env_ref),
            )
        )
    ]
    for i in (0, 1, 4, 3, 2):
        loads[i].start()

    def remote(src, dst, send, receive, s, t):
        return pltpu.make_async_remote_copy(
            src_ref=src, dst_ref=dst, send_sem=send, recv_sem=receive, **at(s, t)
        )

    iso_copy = remote(iso_ref, piso, one_send.at[0], one_recv.at[0], partner, term)
    env_copy = remote(env_ref, left, one_send.at[1], one_recv.at[1], partner, term)
    side_copy = remote(env_ref, came_env, one_send.at[1], one_recv.at[1], partner, term)

    last_whole = remote(last_ref, came, last_send.at[0], last_recv.at[0], partner, term)
    kept = left.shape[1] - rows

    def half_of(site, level, upper):
        return site.at[level, pl.ds(kept, rows) if upper else pl.ds(0, kept)]

    last_parts = [
        remote(
            half_of(last_ref, level, upper),
            half_of(came, level, upper),
            last_send.at[i],
            last_recv.at[i],
            following,
            term,
        )
        for i, (level, upper) in enumerate(
            ((own_level, True), (own_level, False), (1 - own_level, False))
        )
    ]
    share_copy = remote(
        half_of(came, own_level, True),
        half_of(came, own_level, True),
        one_send.at[2],
        last_recv.at[3],
        sec,
        beside,
    )

    def block_of(g):
        return pl.ds(pl.multiple_of(g * rows, rows), rows)

    def fresh_first(k):
        return remote(
            fresh.at[k, pl.ds(0, rows)],
            left.at[k, pl.ds(0, rows)],
            fresh_send.at[0],
            fresh_recv.at[0],
            ahead,
            term,
        )

    def fresh_block(g):
        return remote(
            fresh.at[:, block_of(g)],
            left.at[:, block_of(g)],
            fresh_send.at[0],
            fresh_recv.at[g],
            ahead,
            term,
        )

    def recv_row(n, slot):
        return slot * (1 + n)

    def in_copy(n, x):
        return remote(
            acc.at[n, x],
            recv.at[n, in_slot, x],
            in_send.at[n],
            chunk_recv.at[recv_row(n, in_slot), x],
            sec,
            inward,
        )

    def out_copy(n, x):
        return remote(
            tot.at[n, x],
            recv.at[n, 1, x],
            out_send.at[n],
            chunk_recv.at[recv_row(n, 1), x],
            sec,
            outward,
        )

    def arrived(n, slot, x):
        return remote(
            acc.at[n, x],
            recv.at[n, slot, x],
            in_send.at[n],
            chunk_recv.at[recv_row(n, slot), x],
            sec,
            inward,
        )

    def set_basis(which, source, flip):
        for s in range(PHYS):
            value = source[s]
            turned = value.T
            basis[which, s] = turned if flip else value
            table[which, s] = value if flip else turned
            if s == 1:
                table[which, 2] = -value if flip else -turned

    def extend(values, which, kinds):
        wide = [
            [matmul(value, basis[which, r]).astype(BF16) for r in range(PHYS)] for value in values
        ]
        results = []
        for (wide_0, wide_1), kind in zip(wide, kinds):
            first = jnp.where(kind == 1, 1, jnp.where(kind == 3, 2, 0))
            second = jnp.where(kind == 0, 1, jnp.where(kind == 2, 2, 0))
            result = matmul(table[which, first], wide_0) + matmul(table[which, second], wide_1)
            results.append(result.astype(BF16))
        return results

    group = GROUP if terms % GROUP == 0 else 1
    side_group = SIDE if terms % SIDE == 0 else 1

    def own_group(i, carry):
        members = [group * i + m for m in range(group)]
        kinds = [kind_ref[0, k] for k in members]
        for k, value in zip(members, extend([env_ref[k] for k in members], 0, kinds)):
            mid[k] = value
        return carry

    def split_levels(i):
        sites[i] = jnp.transpose(raw[i], (1, 0, 2))

    loads[0].wait()
    split_levels(0)
    loads[1].wait()
    split_levels(1)

    pl.semaphore_wait(barrier, 3 + jnp.where(has_outward, 1, 0))

    @pl.when(is_odd)
    def _():
        iso_copy.start()
        for copy in last_parts:
            copy.start()

    @pl.when(is_even)
    def _():
        last_whole.start()

    loads[4].wait()

    @pl.when(is_odd)
    def _():
        side_copy.start()

        def turn(k, carry):
            rbuf[k] = env_ref[k].T
            return carry

        lax.fori_loop(0, terms, turn, 0)

    @pl.when(is_even)
    def _():
        env_copy.start()

    loads[3].wait()

    @pl.when(is_even)
    def _():
        set_basis(0, iso_ref, False)
        lax.fori_loop(0, terms // group, own_group, 0)

    @pl.when(is_odd)
    def _():
        loads[2].wait()
        split_levels(2)

    @pl.when(is_even)
    def _():
        iso_copy.wait_recv()
        set_basis(1, piso, False)

        def fresh_group(i, carry):
            members = [group * i + m for m in range(group)]
            kinds = [kind_ref[0, k] for k in members]
            for k, value in zip(members, extend([mid[k] for k in members], 1, kinds)):
                fresh[k] = value
                fresh_first(k).start()
            return carry

        lax.fori_loop(0, terms // group, fresh_group, 0)
        for g in range(1, PARTS):
            fresh_block(g).start()

        def right_group(i, carry):
            members = [side_group * i + m for m in range(side_group)]
            kinds = [kind_ref[1, k] for k in members]
            for k, value in zip(members, extend(extend([came_env[k] for k in members], 3, kinds), 2, kinds)):
                rbuf[k] = value.T

            @pl.when(i == 0)
            def _():
                last_parts[0].wait_recv()
                share_copy.start()

            return carry

        set_basis(2, iso_ref, True)
        set_basis(3, piso, True)
        loads[2].wait()
        split_levels(2)
        side_copy.wait_recv()
        lax.fori_loop(0, terms // side_group, right_group, 0)

    def right_chunk(n, j):
        for k in range(terms):
            h[n, k, lax.rem(j, pairs), block_of(j // pairs)] = matmul(v[j], rbuf[k]).astype(BF16)

    def first_right(i, carry):
        level = jnp.where(is_even, own_level + i - 2 * own_level * i, i)

        @pl.when(jnp.logical_and(is_odd, i == 0))
        def _():
            last_whole.wait_recv()

        @pl.when(jnp.logical_and(is_even, i == 0))
        def _():
            last_parts[1].wait_recv()

        @pl.when(jnp.logical_and(is_even, i > 0))
        def _():
            last_parts[2].wait_recv()
            remote(
                half_of(came, 1 - own_level, True),
                half_of(came, 1 - own_level, True),
                one_send.at[2],
                last_recv.at[3],
                sec,
                beside,
            ).wait_recv()

        for t in range(PHYS):
            x = PHYS * level + t
            value = matmul(came[level], first_ref[t])
            rounded = value.astype(BF16)
            for part in range(PARTS):
                two_site[pairs * part + x] = value[part * rows : (part + 1) * rows]
                v[pairs * part + x] = rounded[part * rows : (part + 1) * rows]
            for k in range(terms):
                h[0, k, x] = matmul(rounded, rbuf[k]).astype(BF16)
        return carry

    lax.fori_loop(0, PHYS, first_right, 0)

    def right_of(n, g):
        lhs = jnp.concatenate([v[pairs * g + x] for x in range(pairs)], axis=0)
        for k in range(terms):
            value = matmul(lhs, rbuf[k]).astype(BF16)
            for x in range(pairs):
                h[n, k, x, block_of(g)] = value[x * rows : (x + 1) * rows]

    @pl.when(is_odd)
    def _():
        env_copy.wait_recv()

    def wait_block(g):
        fresh_block(g).wait_recv()

    def chunk_sum(n, g, s, t):
        total = None
        for k in range(terms):
            kind_0, kind_1 = kind_ref[0, k], kind_ref[1, k]
            flip_0, minus_0 = lax.rem(kind_0, 2), kind_0 // 2
            flip_1, minus_1 = lax.rem(kind_1, 2), kind_1 // 2
            from_s = s + flip_0 - 2 * s * flip_0
            from_t = t + flip_1 - 2 * t * flip_1
            sign = (1 - 2 * s * minus_0) * (1 - 2 * t * minus_1)
            lhs = left[k, block_of(g)] * sign.astype(F32).astype(BF16)
            value = matmul(lhs, h[n, k, PHYS * from_s + from_t])
            total = value if total is None else total + value
        return total.astype(BF16)

    def partial_of(n, g):
        if n == 0:

            @pl.when(is_even)
            def _():
                wait_block(g)

        for s in range(PHYS):
            for t in range(PHYS):
                acc[n, pairs * g + PHYS * s + t] = chunk_sum(n, g, s, t)

    def send_partial(n, j):
        x = lax.rem(j, pairs)
        if n == 0:

            @pl.when(jnp.logical_and(is_even, x == 0))
            def _():
                wait_block(j // pairs)

        acc[n, j] = chunk_sum(n, j // pairs, x // PHYS, lax.rem(x, PHYS))
        in_copy(n, j).start()

    lanes = out_ref.shape[1]
    halves = two_site.shape[2] // lanes
    stride = pairs * halves

    def pass_inward(n, j):
        arrived(n, 0, j).wait_recv()
        acc[n, j] = (acc[n, j].astype(F32) + recv[n, 0, j].astype(F32)).astype(BF16)
        in_copy(n, j).start()

    def pass_outward(n, j, squares):
        arrived(n, 1, j).wait_recv()
        came_in = recv[n, 1, j].astype(F32)
        own = jnp.where(middle, 1.0, 0.0)
        whole = (came_in + own * acc[n, j].astype(F32)).astype(BF16)

        @pl.when(has_outward)
        def _():
            tot[n, j] = whole
            out_copy(n, j).start()

        value = two_site[j] - step_size * whole.astype(F32)
        if n < STEPS - 1:
            two_site[j] = value
            v[j] = value.astype(BF16)
            return squares
        x = lax.rem(j, pairs)
        start = (j // pairs) * (rows * stride) + (x // PHYS) * (halves * PHYS) + lax.rem(x, PHYS)
        for c in range(halves):
            out_ref[pl.ds(start + c * PHYS, rows, stride=stride), :] = value[
                :, c * lanes : (c + 1) * lanes
            ]
        return squares + jnp.sum((value * value).reshape((rows // 8, 8, value.shape[1])), axis=0)

    lag = jnp.where(has_outward, min(LAG, chunks), chunks)
    begin = jnp.where(has_outward, 0, chunks)
    zero = jnp.zeros((8, two_site.shape[2]), F32)
    for n in range(STEPS):
        gated = jnp.logical_and(is_even, has_outward) if n == 0 else False
        ready = jnp.where(is_end, 0, jnp.where(gated, 1, PARTS))
        sending = jnp.where(is_end, chunks, 0)

        def ahead_of(g, carry):
            partial_of(n, g)
            return carry

        def sent(j, carry):
            send_partial(n, j)
            return carry

        def step(j, squares):
            @pl.when(j < chunks)
            def _():
                if n == 0:

                    @pl.when(
                        jnp.logical_and(
                            gated, jnp.logical_and(lax.rem(j, pairs) == 0, j < chunks - pairs)
                        )
                    )
                    def _():
                        partial_of(n, j // pairs + 1)

                pass_inward(n, j)

            return squares

        def body(j, squares):
            squares = step(j, squares)
            done = j - lag
            squares = pass_outward(n, done, squares)
            if n < STEPS - 1:

                late = jnp.logical_and(is_end, done >= chunks - pairs)

                @pl.when(
                    jnp.logical_and(jnp.logical_not(late), lax.rem(done, pairs) == pairs - 1)
                )
                def _():
                    right_of(n + 1, done // pairs)

                @pl.when(late)
                def _():
                    right_chunk(n + 1, done)

            return squares

        lax.fori_loop(0, ready, ahead_of, 0)
        lax.fori_loop(0, sending, sent, 0)
        lax.fori_loop(begin, lag, step, 0)
        squares = lax.fori_loop(lag, chunks + lag, body, zero)

    size = two_site.shape[0] * two_site.shape[1] * two_site.shape[2]
    scale = lax.rsqrt(jnp.full((1, 1), jnp.sum(squares), F32) / size + epsilon)

    out_ref[...] = out_ref[...] * scale


    @pl.when(is_odd)
    def _():
        iso_copy.wait_send()
        for copy in last_parts:
            copy.wait_send()
        side_copy.wait_send()

    @pl.when(is_even)
    def _():
        last_whole.wait_send()
        env_copy.wait_send()
        share_copy.wait_send()

        remote(fresh, left, fresh_send.at[0], fresh_recv.at[0], ahead, term).wait_send()

    for n in range(STEPS):
        remote(
            acc.at[n], recv.at[n, 0], in_send.at[n], chunk_recv.at[0, 0], sec, inward
        ).wait_send()

        @pl.when(has_outward)
        def _():
            remote(
                tot.at[n], recv.at[n, 0], out_send.at[n], chunk_recv.at[0, 0], sec, outward
            ).wait_send()


def shards(n_sec, n_term, meet_env, meet_iso, last_site, first_site, term_kind):
    terms, bond = meet_env.shape[1], meet_env.shape[2]
    pairs = PHYS * PHYS

    vmem = pl.BlockSpec(memory_space=pltpu.VMEM)
    block = (bond, bond)
    chunks = pairs * PARTS
    strip = (bond // PARTS, bond)
    lanes = min(bond, 128)
    dma = pltpu.SemaphoreType.DMA
    out = pl.pallas_call(
        functools.partial(kernel, n_sec, n_term, terms),
        out_shape=jax.ShapeDtypeStruct((pairs * bond * bond // lanes, lanes), F32),
        in_specs=[pl.BlockSpec(memory_space=pltpu.HBM)] * 5,
        out_specs=vmem,
        scratch_shapes=[
            pltpu.SMEM(term_kind.shape[::-1], jnp.int32),
            pltpu.VMEM((terms,) + block, BF16),
            pltpu.VMEM((3, bond, PHYS, bond), BF16),
            pltpu.VMEM((3, PHYS) + block, BF16),
            pltpu.VMEM((terms,) + block, BF16),
            pltpu.VMEM((terms,) + block, BF16),
            pltpu.VMEM((terms,) + block, BF16),
            pltpu.VMEM((terms,) + block, BF16),
            pltpu.VMEM((terms,) + block, BF16),
            pltpu.VMEM((PHYS,) + block, BF16),
            pltpu.VMEM((PHYS,) + block, BF16),
            pltpu.VMEM((4, PHYS) + block, BF16),
            pltpu.VMEM((4, 3) + block, BF16),
            pltpu.VMEM((STEPS, terms, pairs) + block, BF16),
            pltpu.VMEM((chunks,) + strip, BF16),
            pltpu.VMEM((chunks,) + strip, F32),
            pltpu.VMEM((STEPS, chunks) + strip, BF16),
            pltpu.VMEM((STEPS, chunks) + strip, BF16),
            pltpu.VMEM((STEPS, 2, chunks) + strip, BF16),
            dma((5,)),
            dma((3,)),
            dma((2,)),
            dma((3,)),
            dma((4,)),
            dma((1,)),
            dma((PARTS,)),
            dma((STEPS,)),
            dma((1 + STEPS, chunks)),
            dma((STEPS,)),
        ],
        compiler_params=pltpu.CompilerParams(
            collective_id=0, has_side_effects=True, vmem_limit_bytes=48 * 1024 * 1024
        ),
    )(*(pltpu.with_memory_space_constraint(a, pltpu.HBM) for a in (term_kind.T, meet_env[0], meet_iso[0], last_site[0], first_site[0])))
    out = out.reshape(bond, PHYS, bond // lanes, PHYS, lanes)
    out = jnp.transpose(out, (0, 1, 3, 2, 4))
    return out.reshape(1, bond, PHYS, PHYS, bond)


def solution(mesh):
    in_specs = (
        P("sec", "term", None, None),
        P("sec", None, None, None),
        P("sec", None, None, None),
        P("sec", None, None, None),
        P("term", None),
    )
    out_specs = P("sec", None, None, None, None)
    body = functools.partial(shards, mesh.shape["sec"], mesh.shape["term"])
    return jax.shard_map(body, mesh=mesh, in_specs=in_specs, out_specs=out_specs, check_vma=False)
```
